1024 devices in a mesh: tile: 64 (over z, y), slab: 16 (over x, core).
Axes of the slice: x: 8, y: 8, z: 8, core: 2. Of those that a mesh axis runs over, the one named last changes fastest.
Arguments:
- amplitudes: float32 [64, 768, 96], P('tile'), may hold values from -6 to 6
- cholesky: float32 [512, 768, 96], P('slab'), may hold values from -0.12873545 to 0.12873545
- pair_occ: int32 [64, 2], replicated, may hold values from 0 to 63
- hole_integrals: float32 [64, 64], replicated, may hold values from -2 to 2
- other_terms: float32 [64, 768, 96], P('tile', 'slab'), may hold values from -6 to 6
- occ_energy: float32 [64], replicated, may hold values from -2 to -0.4
- vir_energy: float32 [768], replicated, may hold values from 0.2 to 3
Outputs:
- amp_new: float32 [64, 768, 96], P('tile', 'slab')
The draws below stay inside these ranges and needn't reach their ends.
All inputs are finite; a program needn't handle non-finite values.
Results may differ from the reference program's by a relative error of at most 0.0001.
Values sent between devices are 32-bit elements; how exact they have to be, the bound alone decides.
No kernel may reach another device: no remote copies, remote signals or barrier semaphores. Data moves between devices by JAX's collectives and lax.ppermute only.
A program may use at most 32 MiB of HBM per device.

```python
import jax
import jax.numpy as jnp
from jax import lax

O = 64
NV = 768
OB = 8
VB = 96
PAIRS = 64
NQ = 512


def plant(array, key, smallest, largest):
    place = [jax.random.randint(jax.random.fold_in(key, axis), (), 0, length) for axis, length in enumerate(array.shape)]
    main_axis = array.shape.index(max(array.shape))
    next_to = place[:main_axis] + [(place[main_axis] + 1) % array.shape[main_axis]] + place[main_axis + 1:]
    return array.at[tuple(place)].set(smallest).at[tuple(next_to)].set(largest)


def levels(stream_key, extent, shards, smallest, top_value):
    gain, own = 1.0, jax.random.fold_in(stream_key, 6)
    for dim, parts in shards:
        steps = jnp.exp(jax.random.uniform(jax.random.fold_in(own, dim), (parts,), jnp.float32, smallest / len(shards), top_value / len(shards)))
        gain = gain * jnp.repeat(steps, extent[dim] // parts).reshape([-1 if axis == dim else 1 for axis in range(len(extent))])
    return gain


def gaussian(stream_key, extent, scale, most, cuts=(), kind=jnp.bfloat16):
    entries = jax.random.normal(stream_key, extent, jnp.float32) * scale
    if len(cuts) > 0:
        entries = levels(stream_key, extent, cuts, -0.22, 0.18) * entries
    return jnp.clip(entries, min=-most, max=most).astype(kind)


def setup_inputs(seed: int = 0) -> dict:
    key_list = jax.random.split(jax.random.key(seed), 8)
    amplitudes = gaussian(key_list[0], (PAIRS, NV, VB), 1.0, 6.0, ((0, 64),), jnp.float32)
    cholesky = gaussian(key_list[1], (NQ, NV, VB), ((NQ * VB * VB) ** -0.25), 0.12873545, ((0, 16),), jnp.float32)
    pair_occ = plant(jax.random.randint(key_list[2], (PAIRS, 2), 0, O), jax.random.fold_in(key_list[2], 1), 0, O - 1).astype(jnp.int32)
    hole_integrals = gaussian(key_list[3], (PAIRS, PAIRS), (PAIRS // 8) ** -0.5, 2.0, (), jnp.float32)
    other_terms = gaussian(key_list[4], (PAIRS, NV, VB), 1.0, 6.0, ((0, 64), (1, 16)), jnp.float32)
    occ_energy = jnp.clip(jax.random.uniform(key_list[5], (O,), jnp.float32, -2.0, -0.4), -2.0, -0.4)
    vir_energy = jnp.clip(jax.random.uniform(key_list[6], (NV,), jnp.float32, 0.2, 3.0), 0.2, 3.0)
    return dict(amplitudes=amplitudes, cholesky=cholesky, pair_occ=pair_occ, hole_integrals=hole_integrals, other_terms=other_terms, occ_energy=occ_energy, vir_energy=vir_energy)


def reference(amplitudes, cholesky, pair_occ, hole_integrals, other_terms, occ_energy, vir_energy):
    pairs = amplitudes.shape[0]
    irreps = jnp.bitwise_xor(pair_occ[:, 0] // OB, pair_occ[:, 1] // OB).astype(jnp.int32)
    blocks = jnp.arange(8, dtype=jnp.int32)
    partner = jnp.bitwise_xor(blocks[None, :], irreps[:, None]).astype(jnp.int32)
    tiles = amplitudes.reshape(pairs, 8, VB, VB)

    def ladder_step(total, vectors):
        left = vectors.reshape(8, VB, VB)
        right = jnp.take(left, partner, axis=0)
        middle = jnp.einsum("pkcd,pkbd->pkcb", tiles, right, precision=lax.Precision.HIGHEST)
        return total + jnp.einsum("kac,pkcb->pkab", left, middle, precision=lax.Precision.HIGHEST), None

    ladder, _ = lax.scan(ladder_step, jnp.zeros((pairs, 8, VB, VB), jnp.float32), cholesky)
    ladder = ladder.reshape(pairs, NV, VB)
    masked = hole_integrals * (irreps[:, None] == irreps[None, :]).astype(jnp.float32)
    hole = jnp.dot(masked, amplitudes.reshape(pairs, NV * VB), precision=lax.Precision.HIGHEST).reshape(pairs, NV, VB)
    residual = other_terms + ladder + hole
    pair_energy = jnp.take(occ_energy, pair_occ[:, 0]) + jnp.take(occ_energy, pair_occ[:, 1])
    partner_energy = jnp.take(vir_energy.reshape(8, VB), partner, axis=0)
    row_block = (jnp.arange(NV, dtype=jnp.int32) // VB).astype(jnp.int32)
    column_energy = jnp.take(partner_energy, row_block, axis=1)
    denominator = pair_energy[:, None, None] - vir_energy[None, :, None] - column_energy
    return residual / denominator
```

```python
import functools

import jax
import jax.numpy as jnp
from jax import lax
from jax.experimental import pallas as pl
from jax.experimental.pallas import tpu as pltpu
from jax.sharding import PartitionSpec as P

LANES = 128
Y = 8


def split(x):
    high = x.astype(jnp.bfloat16)
    return high, (x - high.astype(jnp.float32)).astype(jnp.bfloat16)


def irrep_of(pair_ref, pair, occ_block):
    return lax.bitwise_xor(
        lax.div(pair_ref[pair, 0], occ_block), lax.div(pair_ref[pair, 1], occ_block)
    )


def head_kernel(amp_t_ref, amp_ref, mine_ref):
    width = amp_t_ref.shape[0]
    rows_dev = mine_ref.shape[1]
    padded = jnp.concatenate(
        [amp_t_ref[...], jnp.zeros((LANES - width, amp_t_ref.shape[1]), jnp.float32)], axis=0
    )
    amp_ref[...] = jnp.transpose(padded)[:, :width]
    start = pl.multiple_of(lax.axis_index("slab") * rows_dev, 8)
    rows = amp_ref[pl.ds(start, rows_dev), :]
    for copy in range(mine_ref.shape[0]):
        mine_ref[copy] = rows


def ladder_kernel(occ_block, pair_ref, amp_ref, vec_ref, out_ref, weight, left, right, total):
    step = pl.program_id(0)
    count, width, rows_all = vec_ref.shape
    irrep = irrep_of(pair_ref, lax.axis_index("tile"), occ_block)

    @pl.when(step == 0)
    def _():
        weight[...] = jnp.zeros_like(weight)
        right[...] = jnp.zeros_like(right)
        total[...] = jnp.zeros_like(total)
        for block in range(8):
            high, low = split(amp_ref[block * width : (block + 1) * width, :])
            for row in (0, LANES):
                weight[block, row : row + width, :width] = high
                weight[block, row : row + width, LANES : LANES + width] = low

    def prepare(q):
        x = vec_ref[q]
        padded = jnp.concatenate([x, jnp.zeros((LANES - width, rows_all), jnp.float32)], axis=0)
        high, low = split(jnp.transpose(padded))
        left[q, :, :LANES] = high
        left[q, :, LANES:] = low
        high, low = split(x)
        for block in range(8):
            columns = slice(block * width, (block + 1) * width)
            right[block, q * LANES : q * LANES + width, :width] = high[:, columns]
            right[block, q * LANES : q * LANES + width, LANES : LANES + width] = low[:, columns]

    for q in range(count):
        prepare(q)

    for block in range(8):
        rows = left[:, block * width : (block + 1) * width, :].reshape(count * width, 2 * LANES)
        both = jnp.dot(rows, weight[block], preferred_element_type=jnp.float32)
        high, low = split(both[:, :LANES] + both[:, LANES:])
        middle = jnp.concatenate(
            [
                jnp.concatenate([part[q * width : (q + 1) * width] for q in range(count)], axis=1)
                for part in (high, low)
            ],
            axis=0,
        )
        total[block] += jnp.dot(
            middle, right[lax.bitwise_xor(block, irrep)], preferred_element_type=jnp.float32
        )

    @pl.when(step == pl.num_programs(0) - 1)
    def _():
        half = width // 2
        for block in range(8):
            value = (
                total[block, :width, :width]
                + total[block, :width, LANES : LANES + width]
                + total[block, width:, :width]
                + total[block, width:, LANES : LANES + width]
            )
            out_ref[2 * block] = value[:half]
            out_ref[2 * block + 1] = value[half:]


def hole_kernel(occ_block, pair_ref, integral_ref, rows_ref, out_ref):
    me = lax.axis_index("tile")
    my_z, my_y = lax.div(me, Y), lax.rem(me, Y)
    tiles = [rows_ref[y] for y in range(Y)]
    sources = [irrep_of(pair_ref, my_z * Y + y, occ_block) for y in range(Y)]
    for z in range(out_ref.shape[0]):
        target = z * Y + my_y
        irrep = irrep_of(pair_ref, target, occ_block)
        value = None
        for y in range(Y):
            factor = jnp.where(irrep == sources[y], integral_ref[target, my_z * Y + y], 0.0)
            term = factor * tiles[y]
            value = term if value is None else value + term
        out_ref[z] = value


def final_kernel(occ_block, pair_ref, occ_ref, vir_ref, other_ref, ladder_ref, hole_ref, out_ref):
    pair = lax.axis_index("tile")
    slab = lax.axis_index("slab")
    rows, width = out_ref.shape
    irrep = irrep_of(pair_ref, pair, occ_block)
    block = lax.div(slab, 2)
    residual = other_ref[...]
    for piece in range(ladder_ref.shape[0]):
        residual = residual + ladder_ref[piece]
    for piece in range(hole_ref.shape[0]):
        residual = residual + hole_ref[piece]
    pair_energy = occ_ref[pair_ref[pair, 0]] + occ_ref[pair_ref[pair, 1]]
    column = vir_ref[pl.ds(lax.bitwise_xor(block, irrep), 1), :]
    own = vir_ref[pl.ds(block, 1), :]
    lane = lax.broadcasted_iota(jnp.int32, (rows, width), 1)
    row = lax.broadcasted_iota(jnp.int32, (rows, width), 0) + lax.rem(slab, 2) * rows
    row_energy = jnp.sum(jnp.where(lane == row, own, 0.0), axis=1, keepdims=True)
    out_ref[...] = residual / (pair_energy - row_energy - column)


def local(amplitudes, cholesky, pair_occ, hole_integrals, other_terms, occ_energy, vir_energy):
    _, rows_all, width = amplitudes.shape
    vectors = cholesky.shape[0]
    slabs = lax.axis_size("slab")
    tiles = lax.axis_size("tile")
    rows_dev = rows_all // slabs
    depth = tiles // Y
    occ_block = occ_energy.shape[0] // 8
    vmem = pl.BlockSpec(memory_space=pltpu.VMEM)
    smem = pl.BlockSpec(memory_space=pltpu.SMEM)
    groups_y = [[z * Y + y for y in range(Y)] for z in range(depth)]
    groups_z = [[z * Y + y for z in range(depth)] for y in range(Y)]

    amp, mine = pl.pallas_call(
        head_kernel,
        out_shape=(
            jax.ShapeDtypeStruct((rows_all, width), jnp.float32),
            jax.ShapeDtypeStruct((Y, rows_dev, width), jnp.float32),
        ),
        in_specs=[vmem],
        out_specs=(vmem, vmem),
        name="head",
    )(jnp.transpose(amplitudes[0]))
    gathered = lax.all_to_all(mine, "tile", 0, 0, axis_index_groups=groups_y, tiled=True)

    chunk = 8
    steps = vectors // chunk
    flops = 2 * vectors * 8 * width * 4 * LANES * LANES * 2
    ladder = pl.pallas_call(
        functools.partial(ladder_kernel, occ_block),
        grid=(steps,),
        out_shape=jax.ShapeDtypeStruct((slabs, rows_dev, width), jnp.float32),
        in_specs=[
            smem,
            pl.BlockSpec((rows_all, width), lambda i: (0, 0)),
            pl.BlockSpec((chunk, width, rows_all), lambda i: (i, 0, 0)),
        ],
        out_specs=pl.BlockSpec((slabs, rows_dev, width), lambda i: (0, 0, 0)),
        scratch_shapes=[
            pltpu.VMEM((8, 2 * LANES, 2 * LANES), jnp.bfloat16),
            pltpu.VMEM((chunk, rows_all, 2 * LANES), jnp.bfloat16),
            pltpu.VMEM((8, chunk * LANES, 2 * LANES), jnp.bfloat16),
            pltpu.VMEM((8, 2 * width, 2 * LANES), jnp.float32),
        ],
        compiler_params=pltpu.CompilerParams(vmem_limit_bytes=40 << 20),
        cost_estimate=pl.CostEstimate(flops=flops, bytes_accessed=cholesky.size * 4, transcendentals=0),
        name="ladder",
    )(pair_occ, amp, jnp.transpose(cholesky, (0, 2, 1)))
    partial = pl.pallas_call(
        functools.partial(hole_kernel, occ_block),
        out_shape=jax.ShapeDtypeStruct((depth, rows_dev, width), jnp.float32),
        in_specs=[smem, smem, vmem],
        out_specs=vmem,
        name="hole",
    )(pair_occ, hole_integrals, gathered)
    hole = lax.all_to_all(partial, "tile", 0, 0, axis_index_groups=groups_z, tiled=True)
    pieces = lax.all_to_all(ladder, "slab", 0, 0, tiled=True)
    out = pl.pallas_call(
        functools.partial(final_kernel, occ_block),
        out_shape=jax.ShapeDtypeStruct((rows_dev, width), jnp.float32),
        in_specs=[smem, smem, vmem, vmem, vmem, vmem],
        out_specs=vmem,
        name="final",
    )(pair_occ, occ_energy, vir_energy.reshape(8, width), other_terms[0], pieces, hole)
    return out[None]


def solution(mesh):
    placed = (
        P("tile", None, None),
        P("slab", None, None),
        P(),
        P(),
        P("tile", "slab", None),
        P(),
        P(),
    )
    return jax.shard_map(
        local, mesh=mesh, in_specs=placed, out_specs=P("tile", "slab", None), check_vma=False
    )
```

```python
import functools

import jax
import jax.numpy as jnp
from jax import lax
from jax.experimental import pallas as pl
from jax.experimental.pallas import tpu as pltpu
from jax.sharding import PartitionSpec as P

LANES = 128
Y = 8


def split(x):
    high = x.astype(jnp.bfloat16)
    return high, (x - high.astype(jnp.float32)).astype(jnp.bfloat16)


def irrep_of(pair_ref, pair, occ_block):
    return lax.bitwise_xor(
        lax.div(pair_ref[0, pair], occ_block), lax.div(pair_ref[1, pair], occ_block)
    )


def head_kernel(amp_t_ref, mine_ref, window, turned, sem):
    width, rows_all = amp_t_ref.shape
    copies, rows_dev, _ = mine_ref.shape
    span = window.shape[1]
    first = lax.axis_index("slab") * rows_dev
    base = jnp.minimum(lax.div(first, LANES) * LANES, rows_all - span)
    load = pltpu.make_async_copy(
        amp_t_ref.at[:, pl.ds(pl.multiple_of(base, LANES), span)], window, sem
    )
    load.start()
    load.wait()
    padded = jnp.concatenate(
        [window[...], jnp.zeros((LANES - width, span), jnp.float32)], axis=0
    )
    turned[...] = jnp.transpose(padded)
    rows = turned[pl.ds(pl.multiple_of(first - base, 8), rows_dev), :width]
    for copy in range(copies):
        mine_ref[copy] = rows


def ladder_kernel(
    occ_block, chunk, offset, pair_ref, amp_t_ref, after_ref, vec_hbm, *refs
):
    base_ref = refs[0] if offset else None
    out_ref, weight, left_even, left_odd, vectors, total, sem = refs[-7:]
    count, width, rows_all = vectors.shape
    chunks = count // chunk
    lefts = (left_even, left_odd)
    irrep = irrep_of(pair_ref, lax.axis_index("tile"), occ_block)
    loads = []
    bounds = list(range(chunk)) + [c * chunk for c in range(1, chunks + 1)]
    for index, (begin, end) in enumerate(zip(bounds[:-1], bounds[1:])):
        loads.append(
            pltpu.make_async_copy(
                vec_hbm.at[pl.ds(offset + begin, end - begin)],
                vectors.at[pl.ds(begin, end - begin)],
                sem.at[index],
            )
        )
        loads[-1].start()
    weight[...] = jnp.zeros_like(weight)
    amp = jnp.transpose(amp_t_ref[...])
    for block in range(8):
        high, low = split(amp[block * width : (block + 1) * width, :])
        for row in (0, LANES):
            weight[block, row : row + width, :width] = high
            weight[block, row : row + width, LANES : LANES + width] = low
    fill = jnp.zeros((LANES - width, rows_all), jnp.bfloat16)

    def prepare(c, q):
        for half, part in enumerate(split(vectors[c * chunk + q])):
            lefts[c % 2][q, :, half * LANES : (half + 1) * LANES] = jnp.transpose(
                jnp.concatenate([part, fill], axis=0)
            )

    def beside(parts):
        return jnp.concatenate(parts, axis=1)

    def first(c, block):
        rows = lefts[c % 2][:, block * width : (block + 1) * width, :]
        both = jnp.dot(
            rows.reshape(chunk * width, 2 * LANES),
            weight[block],
            preferred_element_type=jnp.float32,
        )
        parts = split(both[:, :LANES] + both[:, LANES:])
        return jnp.concatenate(
            [beside([x[q * width : (q + 1) * width] for q in range(chunk)]) for x in parts], axis=0
        )

    def second(c, block, middle):
        begin = pl.multiple_of(lax.bitwise_xor(block, irrep) * width, 16)
        rows = lefts[c % 2][:, pl.ds(begin, width), :]
        other = jnp.concatenate(
            [
                beside([rows[q, :, h * LANES : (h + 1) * LANES] for q in range(chunk)])
                for h in range(2)
            ],
            axis=0,
        )
        value = lax.dot_general(
            middle, other, (((1,), (1,)), ((), ())), preferred_element_type=jnp.float32
        )
        total[block] = value if c == 0 else total[block] + value

    for q in range(chunk):
        loads[q].wait()
        prepare(0, q)
    work = [(c, block) for c in range(chunks) for block in range(8)]
    middle = first(*work[0])
    for index, (c, block) in enumerate(work):
        if c + 1 < chunks:
            if block == 0:
                loads[chunk + c].wait()
            for q in range(block * chunk // 8, (block + 1) * chunk // 8):
                prepare(c + 1, q)
        following = first(*work[index + 1]) if index + 1 < len(work) else None
        second(c, block, middle)
        middle = following
    half = width // 2
    for block in range(8):
        value = (
            total[block, :width, :width]
            + total[block, :width, width:]
            + total[block, width:, :width]
            + total[block, width:, width:]
        )
        for part in range(2):
            rows = value[part * half : (part + 1) * half]
            if offset:
                rows = rows + base_ref[2 * block + part]
            out_ref[2 * block + part] = rows


def hole_kernel(occ_block, pair_ref, integral_ref, rows_ref, out_ref):
    me = lax.axis_index("tile")
    my_z, my_y = lax.div(me, Y), lax.rem(me, Y)
    tiles = [rows_ref[y] for y in range(Y)]
    sources = [irrep_of(pair_ref, my_z * Y + y, occ_block) for y in range(Y)]
    for z in range(out_ref.shape[0]):
        target = z * Y + my_y
        irrep = irrep_of(pair_ref, target, occ_block)
        value = None
        for y in range(Y):
            factor = jnp.where(irrep == sources[y], integral_ref[target, my_z * Y + y], 0.0)
            term = factor * tiles[y]
            value = term if value is None else value + term
        out_ref[z] = value


def final_kernel(occ_block, pair_ref, occ_ref, vir_ref, other_ref, ladder_ref, hole_ref, out_ref):
    pair = lax.axis_index("tile")
    slab = lax.axis_index("slab")
    rows, width = out_ref.shape
    irrep = irrep_of(pair_ref, pair, occ_block)
    block = lax.div(slab, 2)
    residual = other_ref[...]
    for piece in range(ladder_ref.shape[0]):
        residual = residual + ladder_ref[piece]
    for piece in range(hole_ref.shape[0]):
        residual = residual + hole_ref[piece]
    pair_energy = occ_ref[pair_ref[0, pair]] + occ_ref[pair_ref[1, pair]]
    column = vir_ref[pl.ds(lax.bitwise_xor(block, irrep), 1), :]
    own = vir_ref[pl.ds(block, 1), :]
    lane = lax.broadcasted_iota(jnp.int32, (rows, width), 1)
    row = lax.broadcasted_iota(jnp.int32, (rows, width), 0) + lax.rem(slab, 2) * rows
    row_energy = jnp.sum(jnp.where(lane == row, own, 0.0), axis=1, keepdims=True)
    out_ref[...] = residual / (pair_energy - row_energy - column)


def local(amplitudes, cholesky, pair_occ, hole_integrals, other_terms, occ_energy, vir_energy):
    _, rows_all, width = amplitudes.shape
    vectors = cholesky.shape[0]
    slabs = lax.axis_size("slab")
    tiles = lax.axis_size("tile")
    rows_dev = rows_all // slabs
    depth = tiles // Y
    occ_block = occ_energy.shape[0] // 8
    vmem = pl.BlockSpec(memory_space=pltpu.VMEM)
    smem = pl.BlockSpec(memory_space=pltpu.SMEM)
    groups_y = [[z * Y + y for y in range(Y)] for z in range(depth)]
    groups_z = [[z * Y + y for z in range(depth)] for y in range(Y)]

    hbm = pl.BlockSpec(memory_space=pltpu.MemorySpace.HBM)
    small = pltpu.CompilerParams(vmem_limit_bytes=6 << 20)
    pairs = jnp.transpose(pair_occ)
    amp_t = jnp.transpose(amplitudes[0])
    vectors_t = jnp.transpose(cholesky, (0, 2, 1))

    mine = pl.pallas_call(
        head_kernel,
        out_shape=jax.ShapeDtypeStruct((Y, rows_dev, width), jnp.float32),
        in_specs=[hbm],
        out_specs=vmem,
        scratch_shapes=[
            pltpu.VMEM((width, 2 * LANES), jnp.float32),
            pltpu.VMEM((2 * LANES, LANES), jnp.float32),
            pltpu.SemaphoreType.DMA,
        ],
        compiler_params=pltpu.CompilerParams(vmem_limit_bytes=60 << 20),
        name="head",
    )(amp_t)
    gathered = lax.all_to_all(mine, "tile", 0, 0, axis_index_groups=groups_y, tiled=True)

    chunk = 8
    share = vectors // 2

    def ladder_part(offset, after, *base):
        flops = 2 * share * 8 * width * (2 * LANES) * (2 * LANES) * 2
        return pl.pallas_call(
            functools.partial(ladder_kernel, occ_block, chunk, offset),
            out_shape=jax.ShapeDtypeStruct((slabs, rows_dev, width), jnp.float32),
            in_specs=[smem, vmem, pl.BlockSpec(memory_space=pl.ANY), hbm] + [vmem] * len(base),
            out_specs=vmem,
            scratch_shapes=[
                pltpu.VMEM((8, 2 * LANES, 2 * LANES), jnp.bfloat16),
                pltpu.VMEM((chunk, rows_all, 2 * LANES), jnp.bfloat16),
                pltpu.VMEM((chunk, rows_all, 2 * LANES), jnp.bfloat16),
                pltpu.VMEM((share, width, rows_all), jnp.float32),
                pltpu.VMEM((8, 2 * width, 2 * width), jnp.float32),
                pltpu.SemaphoreType.DMA((chunk + share // chunk - 1,)),
            ],
            compiler_params=pltpu.CompilerParams(vmem_limit_bytes=58 << 20),
            cost_estimate=pl.CostEstimate(
                flops=flops, bytes_accessed=share * rows_all * width * 4, transcendentals=0
            ),
            name="ladder",
        )(pairs, amp_t, after, vectors_t, *base)

    ladder = ladder_part(0, mine)
    gathered, ladder = lax.optimization_barrier((gathered, ladder))
    partial = pl.pallas_call(
        functools.partial(hole_kernel, occ_block),
        out_shape=jax.ShapeDtypeStruct((depth, rows_dev, width), jnp.float32),
        in_specs=[smem, smem, vmem],
        out_specs=vmem,
        compiler_params=small,
        name="hole",
    )(pairs, hole_integrals, gathered)
    ladder = ladder_part(share, partial, ladder)
    pieces = lax.all_to_all(ladder, "slab", 0, 0, tiled=True)
    hole = lax.all_to_all(partial, "tile", 0, 0, axis_index_groups=groups_z, tiled=True)
    out = pl.pallas_call(
        functools.partial(final_kernel, occ_block),
        out_shape=jax.ShapeDtypeStruct((rows_dev, width), jnp.float32),
        in_specs=[smem, smem, vmem, vmem, vmem, vmem],
        out_specs=vmem,
        compiler_params=small,
        name="final",
    )(pairs, occ_energy, vir_energy.reshape(8, width), other_terms[0], pieces, hole)
    return out[None]


def solution(mesh):
    placed = (
        P("tile", None, None),
        P("slab", None, None),
        P(),
        P(),
        P("tile", "slab", None),
        P(),
        P(),
    )
    return jax.shard_map(
        local, mesh=mesh, in_specs=placed, out_specs=P("tile", "slab", None), check_vma=False
    )
```

```python
import functools

import jax
import jax.numpy as jnp
from jax import lax
from jax.experimental import pallas as pl
from jax.experimental.pallas import tpu as pltpu
from jax.sharding import PartitionSpec as P

LANES = 128
Y = 8
SIZES = (4, 8, 4)


def split(x):
    high = x.astype(jnp.bfloat16)
    return high, (x - high.astype(jnp.float32)).astype(jnp.bfloat16)


def irrep_of(pair_ref, pair, occ_block):
    return lax.bitwise_xor(
        lax.div(pair_ref[0, pair], occ_block), lax.div(pair_ref[1, pair], occ_block)
    )


def pack(ref, rows):
    height, width = rows.shape
    spare = LANES - width
    ref[:, width:] = jnp.zeros((height - 8, spare), jnp.float32)
    ref[:, :width] = rows[: height - 8]
    for part in range(width // spare):
        ref[part * 8 : part * 8 + 8, width:] = rows[
            height - 8 :, part * spare : (part + 1) * spare
        ]


def unpack(tile, width):
    spare = LANES - width
    last = [tile[part * 8 : part * 8 + 8, width:] for part in range(width // spare)]
    return jnp.concatenate([tile[:, :width], jnp.concatenate(last, axis=1)], axis=0)


def head_kernel(amp_t_ref, mine_ref, window, turned, sem):
    width, rows_all = amp_t_ref.shape
    copies = mine_ref.shape[0]
    rows_dev = mine_ref.shape[1] + 8
    span = window.shape[1]
    first = lax.axis_index("slab") * rows_dev
    base = jnp.minimum(lax.div(first, LANES) * LANES, rows_all - span)
    load = pltpu.make_async_copy(
        amp_t_ref.at[:, pl.ds(pl.multiple_of(base, LANES), span)], window, sem
    )
    load.start()
    load.wait()
    padded = jnp.concatenate(
        [window[...], jnp.zeros((LANES - width, span), jnp.float32)], axis=0
    )
    turned[...] = jnp.transpose(padded)
    rows = turned[pl.ds(pl.multiple_of(first - base, 8), rows_dev), :width]
    for copy in range(copies):
        pack(mine_ref.at[copy], rows)


def ladder_kernel(occ_block, sizes, offset, pair_ref, after_ref, amp_hbm, vec_hbm, *refs):
    base_hbm = refs[0] if offset else None
    out_ref, weight, left_even, left_odd, amp_t, base, vectors, total, sem = refs[-9:]
    _, width, rows_all = vectors.shape
    lefts = (left_even, left_odd)
    starts = [sum(sizes[:c]) for c in range(len(sizes))]
    irrep = irrep_of(pair_ref, lax.axis_index("tile"), occ_block)
    pieces = [(q, 1) for q in range(sizes[0])] + list(zip(starts[1:], sizes[1:]))
    load_amp = pltpu.make_async_copy(amp_hbm, amp_t, sem.at[len(pieces)])
    load_amp.start()
    loads = [
        pltpu.make_async_copy(
            vec_hbm.at[pl.ds(offset + begin, size)], vectors.at[pl.ds(begin, size)], sem.at[index]
        )
        for index, (begin, size) in enumerate(pieces)
    ]
    for load in loads:
        load.start()
    if offset:
        load_base = pltpu.make_async_copy(base_hbm, base, sem.at[len(pieces) + 1])
        load_base.start()
    weight[...] = jnp.zeros_like(weight)
    fill = jnp.zeros((LANES - width, rows_all), jnp.bfloat16)

    def prepare(c, q):
        for half, part in enumerate(split(vectors[starts[c] + q])):
            lefts[c % 2][q, :, half * LANES : (half + 1) * LANES] = jnp.transpose(
                jnp.concatenate([part, fill], axis=0)
            )

    def beside(parts):
        return jnp.concatenate(parts, axis=1)

    def first(c, block):
        size = sizes[c]
        rows = lefts[c % 2][:size, block * width : (block + 1) * width, :]
        both = jnp.dot(
            rows.reshape(size * width, 2 * LANES),
            weight[block],
            preferred_element_type=jnp.float32,
        )
        parts = split(both[:, :LANES] + both[:, LANES:])
        return jnp.concatenate(
            [beside([x[q * width : (q + 1) * width] for q in range(size)]) for x in parts], axis=0
        )

    def second(c, block, middle):
        size = sizes[c]
        begin = pl.multiple_of(lax.bitwise_xor(block, irrep) * width, 16)
        rows = lefts[c % 2][:size, pl.ds(begin, width), :]
        other = jnp.concatenate(
            [
                beside([rows[q, :, h * LANES : (h + 1) * LANES] for q in range(size)])
                for h in range(2)
            ],
            axis=0,
        )
        value = lax.dot_general(
            middle, other, (((1,), (1,)), ((), ())), preferred_element_type=jnp.float32
        )
        total[block] = value if c == 0 else total[block] + value

    load_amp.wait()
    amp = jnp.transpose(amp_t[...])
    for block in range(8):
        high, low = split(amp[block * width : (block + 1) * width, :])
        for row in (0, LANES):
            weight[block, row : row + width, :width] = high
            weight[block, row : row + width, LANES : LANES + width] = low
    for q in range(sizes[0]):
        loads[q].wait()
        prepare(0, q)
    work = [(c, block) for c in range(len(sizes)) for block in range(8)]
    middle = first(*work[0])
    for index, (c, block) in enumerate(work):
        if c + 1 < len(sizes):
            size = sizes[c + 1]
            if block == 0:
                loads[sizes[0] + c].wait()
            for q in range(block * size // 8, (block + 1) * size // 8):
                prepare(c + 1, q)
        following = first(*work[index + 1]) if index + 1 < len(work) else None
        second(c, block, middle)
        middle = following
    if offset:
        load_base.wait()
    half = width // 2
    for block in range(8):
        value = (
            total[block, :width, :width]
            + total[block, :width, width:]
            + total[block, width:, :width]
            + total[block, width:, width:]
        )
        for part in range(2):
            piece = 2 * block + part
            pack(out_ref.at[piece], value[part * half : (part + 1) * half])
            if offset:
                out_ref[piece] = out_ref[piece] + base[piece]


def hole_kernel(occ_block, pair_ref, integral_ref, rows_ref, out_ref):
    me = lax.axis_index("tile")
    my_z, my_y = lax.div(me, Y), lax.rem(me, Y)
    tiles = [rows_ref[y] for y in range(Y)]
    sources = [irrep_of(pair_ref, my_z * Y + y, occ_block) for y in range(Y)]
    for z in range(out_ref.shape[0]):
        target = z * Y + my_y
        irrep = irrep_of(pair_ref, target, occ_block)
        value = None
        for y in range(Y):
            factor = jnp.where(irrep == sources[y], integral_ref[target, my_z * Y + y], 0.0)
            term = factor * tiles[y]
            value = term if value is None else value + term
        out_ref[z] = value


def final_kernel(occ_block, pair_ref, occ_ref, vir_ref, other_ref, ladder_ref, hole_ref, out_ref):
    pair = lax.axis_index("tile")
    slab = lax.axis_index("slab")
    rows, width = out_ref.shape
    irrep = irrep_of(pair_ref, pair, occ_block)
    block = lax.div(slab, 2)
    moved = ladder_ref[0]
    for piece in range(1, ladder_ref.shape[0]):
        moved = moved + ladder_ref[piece]
    for piece in range(hole_ref.shape[0]):
        moved = moved + hole_ref[piece]
    residual = other_ref[...] + unpack(moved, width)
    pair_energy = occ_ref[pair_ref[0, pair]] + occ_ref[pair_ref[1, pair]]
    column = vir_ref[pl.ds(lax.bitwise_xor(block, irrep), 1), :]
    own = vir_ref[pl.ds(block, 1), :]
    lane = lax.broadcasted_iota(jnp.int32, (rows, width), 1)
    row = lax.broadcasted_iota(jnp.int32, (rows, width), 0) + lax.rem(slab, 2) * rows
    row_energy = jnp.sum(jnp.where(lane == row, own, 0.0), axis=1, keepdims=True)
    out_ref[...] = residual / (pair_energy - row_energy - column)


def local(amplitudes, cholesky, pair_occ, hole_integrals, other_terms, occ_energy, vir_energy):
    _, rows_all, width = amplitudes.shape
    vectors = cholesky.shape[0]
    slabs = lax.axis_size("slab")
    tiles = lax.axis_size("tile")
    rows_dev = rows_all // slabs
    depth = tiles // Y
    packed = (rows_dev - 8, LANES)
    occ_block = occ_energy.shape[0] // 8
    vmem = pl.BlockSpec(memory_space=pltpu.VMEM)
    smem = pl.BlockSpec(memory_space=pltpu.SMEM)
    groups_y = [[z * Y + y for y in range(Y)] for z in range(depth)]
    groups_z = [[z * Y + y for z in range(depth)] for y in range(Y)]

    hbm = pl.BlockSpec(memory_space=pltpu.MemorySpace.HBM)
    small = pltpu.CompilerParams(vmem_limit_bytes=6 << 20)
    pairs = jnp.transpose(pair_occ)
    amp_t = jnp.transpose(amplitudes[0])
    vectors_t = jnp.transpose(cholesky, (0, 2, 1))

    mine = pl.pallas_call(
        head_kernel,
        out_shape=jax.ShapeDtypeStruct((Y,) + packed, jnp.float32),
        in_specs=[hbm],
        out_specs=vmem,
        scratch_shapes=[
            pltpu.VMEM((width, 2 * LANES), jnp.float32),
            pltpu.VMEM((2 * LANES, LANES), jnp.float32),
            pltpu.SemaphoreType.DMA,
        ],
        compiler_params=pltpu.CompilerParams(vmem_limit_bytes=60 << 20),
        name="head",
    )(amp_t)
    gathered = lax.all_to_all(mine, "tile", 0, 0, axis_index_groups=groups_y, tiled=True)

    sizes = SIZES
    share = vectors // 2

    def ladder_part(offset, after, *base):
        flops = 2 * share * 8 * width * (2 * LANES) * (2 * LANES) * 2
        return pl.pallas_call(
            functools.partial(ladder_kernel, occ_block, sizes, offset),
            out_shape=jax.ShapeDtypeStruct((slabs,) + packed, jnp.float32),
            in_specs=[smem, hbm, hbm, hbm] + [hbm] * len(base),
            out_specs=vmem,
            scratch_shapes=[
                pltpu.VMEM((8, 2 * LANES, 2 * LANES), jnp.bfloat16),
                pltpu.VMEM((max(sizes[::2]), rows_all, 2 * LANES), jnp.bfloat16),
                pltpu.VMEM((max(sizes[1::2]), rows_all, 2 * LANES), jnp.bfloat16),
                pltpu.VMEM((width, rows_all), jnp.float32),
                pltpu.VMEM((slabs,) + packed, jnp.float32),
                pltpu.VMEM((share, width, rows_all), jnp.float32),
                pltpu.VMEM((8, 2 * width, 2 * width), jnp.float32),
                pltpu.SemaphoreType.DMA((sizes[0] + len(sizes) + 1,)),
            ],
            compiler_params=pltpu.CompilerParams(vmem_limit_bytes=58 << 20),
            cost_estimate=pl.CostEstimate(
                flops=flops, bytes_accessed=share * rows_all * width * 4, transcendentals=0
            ),
            name="ladder",
        )(pairs, after, amp_t, vectors_t, *base)

    ladder = ladder_part(0, mine)
    gathered, ladder = lax.optimization_barrier((gathered, ladder))
    partial = pl.pallas_call(
        functools.partial(hole_kernel, occ_block),
        out_shape=jax.ShapeDtypeStruct((depth,) + packed, jnp.float32),
        in_specs=[smem, smem, vmem],
        out_specs=vmem,
        compiler_params=small,
        name="hole",
    )(pairs, hole_integrals, gathered)
    ladder = ladder_part(share, partial, ladder)
    vir = vir_energy.reshape(8, width)
    ladder, vir = lax.optimization_barrier((ladder, vir))
    pieces = lax.all_to_all(ladder, "slab", 0, 0, tiled=True)
    hole = lax.all_to_all(partial, "tile", 0, 0, axis_index_groups=groups_z, tiled=True)
    out = pl.pallas_call(
        functools.partial(final_kernel, occ_block),
        out_shape=jax.ShapeDtypeStruct((rows_dev, width), jnp.float32),
        in_specs=[smem, smem, vmem, vmem, vmem, vmem],
        out_specs=vmem,
        compiler_params=small,
        name="final",
    )(pairs, occ_energy, vir, other_terms[0], pieces, hole)
    return out[None]


def solution(mesh):
    placed = (
        P("tile", None, None),
        P("slab", None, None),
        P(),
        P(),
        P("tile", "slab", None),
        P(),
        P(),
    )
    return jax.shard_map(
        local, mesh=mesh, in_specs=placed, out_specs=P("tile", "slab", None), check_vma=False
    )
```

```python
import functools

import jax
import jax.numpy as jnp
from jax import lax
from jax.experimental import pallas as pl
from jax.experimental.pallas import tpu as pltpu
from jax.sharding import PartitionSpec as P

LANES = 128
Y = 8
SIZES = (2, 6, 8, 8, 8)
CLASSES = 4


def split(x):
    high = x.astype(jnp.bfloat16)
    return high, (x - high.astype(jnp.float32)).astype(jnp.bfloat16)


def irrep_of(pair_ref, pair, occ_block):
    return lax.bitwise_xor(
        lax.div(pair_ref[0, pair], occ_block), lax.div(pair_ref[1, pair], occ_block)
    )


def pack(ref, rows):
    height, width = rows.shape
    spare = LANES - width
    ref[:, width:] = jnp.zeros((height - 8, spare), jnp.float32)
    ref[:, :width] = rows[: height - 8]
    for part in range(width // spare):
        ref[part * 8 : part * 8 + 8, width:] = rows[
            height - 8 :, part * spare : (part + 1) * spare
        ]


def unpack(tile, width):
    spare = LANES - width
    last = [tile[part * 8 : part * 8 + 8, width:] for part in range(width // spare)]
    return jnp.concatenate([tile[:, :width], jnp.concatenate(last, axis=1)], axis=0)


def head_kernel(amp_t_ref, mine_ref, window, turned, sem):
    width, rows_all = amp_t_ref.shape
    copies = mine_ref.shape[0]
    rows_dev = mine_ref.shape[1] + 8
    span = window.shape[1]
    first = lax.axis_index("slab") * rows_dev
    base = jnp.minimum(lax.div(first, LANES) * LANES, rows_all - span)
    load = pltpu.make_async_copy(
        amp_t_ref.at[:, pl.ds(pl.multiple_of(base, LANES), span)], window, sem
    )
    load.start()
    load.wait()
    padded = jnp.concatenate(
        [window[...], jnp.zeros((LANES - width, span), jnp.float32)], axis=0
    )
    turned[...] = jnp.transpose(padded)
    rows = turned[pl.ds(pl.multiple_of(first - base, 8), rows_dev), :width]
    for copy in range(copies):
        pack(mine_ref.at[copy], rows)


def ladder_kernel(
    occ_block, sizes, pair_ref, after_ref, amp_hbm, vec_hbm, out_ref,
    weight, left_even, left_odd, amp_t, vectors, total, sem,
):
    _, width, rows_all = vectors.shape
    lefts = (left_even, left_odd)
    starts = [sum(sizes[:c]) for c in range(len(sizes))]
    irrep = irrep_of(pair_ref, lax.axis_index("tile"), occ_block)
    pieces = [(q, 1) for q in range(sizes[0])] + list(zip(starts[1:], sizes[1:]))
    load_amp = pltpu.make_async_copy(amp_hbm, amp_t, sem.at[len(pieces)])
    load_amp.start()
    loads = [
        pltpu.make_async_copy(
            vec_hbm.at[pl.ds(begin, size)], vectors.at[pl.ds(begin, size)], sem.at[index]
        )
        for index, (begin, size) in enumerate(pieces)
    ]
    for load in loads:
        load.start()
    weight[...] = jnp.zeros_like(weight)
    fill = jnp.zeros((LANES - width, rows_all), jnp.bfloat16)

    def prepare(c, q):
        for half, part in enumerate(split(vectors[starts[c] + q])):
            lefts[c % 2][q, :, half * LANES : (half + 1) * LANES] = jnp.transpose(
                jnp.concatenate([part, fill], axis=0)
            )

    def beside(parts):
        return jnp.concatenate(parts, axis=1)

    def first(c, block):
        size = sizes[c]
        rows = lefts[c % 2][:size, block * width : (block + 1) * width, :]
        both = jnp.dot(
            rows.reshape(size * width, 2 * LANES),
            weight[block],
            preferred_element_type=jnp.float32,
        )
        parts = split(both[:, :LANES] + both[:, LANES:])
        return jnp.concatenate(
            [beside([x[q * width : (q + 1) * width] for q in range(size)]) for x in parts], axis=0
        )

    def second(c, block, middle):
        size = sizes[c]
        begin = pl.multiple_of(lax.bitwise_xor(block, irrep) * width, 16)
        rows = lefts[c % 2][:size, pl.ds(begin, width), :]
        other = jnp.concatenate(
            [
                beside([rows[q, :, h * LANES : (h + 1) * LANES] for q in range(size)])
                for h in range(2)
            ],
            axis=0,
        )
        value = lax.dot_general(
            middle, other, (((1,), (1,)), ((), ())), preferred_element_type=jnp.float32
        )
        total[block] = value if c == 0 else total[block] + value

    load_amp.wait()
    amp = jnp.transpose(amp_t[...])
    for block in range(8):
        high, low = split(amp[block * width : (block + 1) * width, :])
        for row in (0, LANES):
            weight[block, row : row + width, :width] = high
            weight[block, row : row + width, LANES : LANES + width] = low
    for q in range(sizes[0]):
        loads[q].wait()
        prepare(0, q)
    work = [(c, block) for c in range(len(sizes)) for block in range(8)]
    middle = first(*work[0])
    for index, (c, block) in enumerate(work):
        if c + 1 < len(sizes):
            size = sizes[c + 1]
            if block == 0:
                loads[sizes[0] + c].wait()
            for q in range(block * size // 8, (block + 1) * size // 8):
                prepare(c + 1, q)
        following = first(*work[index + 1]) if index + 1 < len(work) else None
        second(c, block, middle)
        middle = following
    half = width // 2
    for block in range(8):
        value = (
            total[block, :width, :width]
            + total[block, :width, width:]
            + total[block, width:, :width]
            + total[block, width:, width:]
        )
        for part in range(2):
            piece = 2 * block + part
            pack(out_ref.at[piece], value[part * half : (part + 1) * half])


def hole_kernel(occ_block, pair_ref, integral_ref, rows_ref, *out_refs):
    me = lax.axis_index("tile")
    my_z, my_y = lax.div(me, Y), lax.rem(me, Y)
    low = lax.rem(my_z, CLASSES)
    count = rows_ref.shape[0]
    sources = [(low + CLASSES * (i // Y)) * Y + i % Y for i in range(count)]
    irreps = [irrep_of(pair_ref, source, occ_block) for source in sources]
    for step, out_ref in enumerate(out_refs):
        target = lax.bitwise_xor(my_z, step) * Y + my_y
        irrep = irrep_of(pair_ref, target, occ_block)
        value = None
        for i in range(count):
            factor = jnp.where(irrep == irreps[i], integral_ref[target, sources[i]], 0.0)
            term = factor * rows_ref[i]
            value = term if value is None else value + term
        out_ref[...] = value


def final_kernel(occ_block, pair_ref, occ_ref, vir_ref, other_ref, ladder_ref, *refs):
    out_ref = refs[-1]
    pair = lax.axis_index("tile")
    slab = lax.axis_index("slab")
    rows, width = out_ref.shape
    irrep = irrep_of(pair_ref, pair, occ_block)
    block = lax.div(slab, 2)
    moved = ladder_ref[0]
    for piece in range(1, ladder_ref.shape[0]):
        moved = moved + ladder_ref[piece]
    for hole_ref in refs[:-1]:
        moved = moved + hole_ref[...]
    residual = other_ref[...] + unpack(moved, width)
    pair_energy = occ_ref[pair_ref[0, pair]] + occ_ref[pair_ref[1, pair]]
    column = vir_ref[pl.ds(lax.bitwise_xor(block, irrep), 1), :]
    own = vir_ref[pl.ds(block, 1), :]
    lane = lax.broadcasted_iota(jnp.int32, (rows, width), 1)
    row = lax.broadcasted_iota(jnp.int32, (rows, width), 0) + lax.rem(slab, 2) * rows
    row_energy = jnp.sum(jnp.where(lane == row, own, 0.0), axis=1, keepdims=True)
    out_ref[...] = residual / (pair_energy - row_energy - column)


def local(amplitudes, cholesky, pair_occ, hole_integrals, other_terms, occ_energy, vir_energy):
    _, rows_all, width = amplitudes.shape
    vectors = cholesky.shape[0]
    slabs = lax.axis_size("slab")
    tiles = lax.axis_size("tile")
    rows_dev = rows_all // slabs
    depth = tiles // Y
    packed = (rows_dev - 8, LANES)
    occ_block = occ_energy.shape[0] // 8
    vmem = pl.BlockSpec(memory_space=pltpu.VMEM)
    smem = pl.BlockSpec(memory_space=pltpu.SMEM)
    spread = depth // CLASSES
    groups = [
        [(low + CLASSES * far) * Y + y for far in range(spread) for y in range(Y)]
        for low in range(CLASSES)
    ]

    hbm = pl.BlockSpec(memory_space=pltpu.MemorySpace.HBM)
    small = pltpu.CompilerParams(vmem_limit_bytes=6 << 20)
    pairs = jnp.transpose(pair_occ)
    amp_t = jnp.transpose(amplitudes[0])
    vectors_t = jnp.transpose(cholesky, (0, 2, 1))

    mine = pl.pallas_call(
        head_kernel,
        out_shape=jax.ShapeDtypeStruct((spread * Y,) + packed, jnp.float32),
        in_specs=[hbm],
        out_specs=vmem,
        scratch_shapes=[
            pltpu.VMEM((width, 2 * LANES), jnp.float32),
            pltpu.VMEM((2 * LANES, LANES), jnp.float32),
            pltpu.SemaphoreType.DMA,
        ],
        compiler_params=pltpu.CompilerParams(vmem_limit_bytes=60 << 20),
        name="head",
    )(amp_t)
    gathered = lax.all_to_all(mine, "tile", 0, 0, axis_index_groups=groups, tiled=True)

    sizes = SIZES
    flops = 2 * vectors * 8 * width * (2 * LANES) * (2 * LANES) * 2
    ladder = pl.pallas_call(
        functools.partial(ladder_kernel, occ_block, sizes),
        out_shape=jax.ShapeDtypeStruct((slabs,) + packed, jnp.float32),
        in_specs=[smem, hbm, hbm, hbm],
        out_specs=vmem,
        scratch_shapes=[
            pltpu.VMEM((8, 2 * LANES, 2 * LANES), jnp.bfloat16),
            pltpu.VMEM((max(sizes[::2]), rows_all, 2 * LANES), jnp.bfloat16),
            pltpu.VMEM((max(sizes[1::2]), rows_all, 2 * LANES), jnp.bfloat16),
            pltpu.VMEM((width, rows_all), jnp.float32),
            pltpu.VMEM((vectors, width, rows_all), jnp.float32),
            pltpu.VMEM((8, 2 * width, 2 * width), jnp.float32),
            pltpu.SemaphoreType.DMA((sizes[0] + len(sizes),)),
        ],
        compiler_params=pltpu.CompilerParams(vmem_limit_bytes=58 << 20),
        cost_estimate=pl.CostEstimate(
            flops=flops, bytes_accessed=cholesky.size * 4, transcendentals=0
        ),
        name="ladder",
    )(pairs, mine, amp_t, vectors_t)
    pieces = lax.all_to_all(ladder, "slab", 0, 0, tiled=True)
    gathered, _ = lax.optimization_barrier((gathered, ladder))
    partial = pl.pallas_call(
        functools.partial(hole_kernel, occ_block),
        out_shape=[jax.ShapeDtypeStruct(packed, jnp.float32)] * CLASSES,
        in_specs=[smem, smem, vmem],
        out_specs=[vmem] * CLASSES,
        compiler_params=small,
        name="hole",
    )(pairs, hole_integrals, gathered)
    hole = [partial[0]]
    for step in range(1, CLASSES):
        route = [(z * Y + y, (z ^ step) * Y + y) for z in range(depth) for y in range(Y)]
        hole.append(lax.ppermute(partial[step], "tile", route))
    out = pl.pallas_call(
        functools.partial(final_kernel, occ_block),
        out_shape=jax.ShapeDtypeStruct((rows_dev, width), jnp.float32),
        in_specs=[smem, smem] + [vmem] * (3 + CLASSES),
        out_specs=vmem,
        compiler_params=small,
        name="final",
    )(pairs, occ_energy, vir_energy.reshape(8, width), other_terms[0], pieces, *hole)
    return out[None]


def solution(mesh):
    placed = (
        P("tile", None, None),
        P("slab", None, None),
        P(),
        P(),
        P("tile", "slab", None),
        P(),
        P(),
    )
    return jax.shard_map(
        local, mesh=mesh, in_specs=placed, out_specs=P("tile", "slab", None), check_vma=False
    )
```

```python
import functools

import jax
import jax.numpy as jnp
from jax import lax
from jax.experimental import pallas as pl
from jax.experimental.pallas import tpu as pltpu
from jax.sharding import PartitionSpec as P

LANES = 128
Y = 8
SIZES = (2, 6, 8, 8, 8)
NEAR = 2


def split(x):
    high = x.astype(jnp.bfloat16)
    return high, (x - high.astype(jnp.float32)).astype(jnp.bfloat16)


def irrep_of(pair_ref, pair, occ_block):
    return lax.bitwise_xor(
        lax.div(pair_ref[0, pair], occ_block), lax.div(pair_ref[1, pair], occ_block)
    )


def pack(ref, rows):
    height, width = rows.shape
    spare = LANES - width
    ref[:, width:] = jnp.zeros((height - 8, spare), jnp.float32)
    ref[:, :width] = rows[: height - 8]
    for part in range(width // spare):
        ref[part * 8 : part * 8 + 8, width:] = rows[
            height - 8 :, part * spare : (part + 1) * spare
        ]


def unpack(tile, width):
    spare = LANES - width
    last = [tile[part * 8 : part * 8 + 8, width:] for part in range(width // spare)]
    return jnp.concatenate([tile[:, :width], jnp.concatenate(last, axis=1)], axis=0)


def head_kernel(amp_t_ref, mine_ref, window, turned, sem):
    width, rows_all = amp_t_ref.shape
    copies = mine_ref.shape[0]
    rows_dev = mine_ref.shape[1] + 8
    span = window.shape[1]
    first = lax.axis_index("slab") * rows_dev
    base = jnp.minimum(lax.div(first, LANES) * LANES, rows_all - span)
    load = pltpu.make_async_copy(
        amp_t_ref.at[:, pl.ds(pl.multiple_of(base, LANES), span)], window, sem
    )
    load.start()
    load.wait()
    padded = jnp.concatenate(
        [window[...], jnp.zeros((LANES - width, span), jnp.float32)], axis=0
    )
    turned[...] = jnp.transpose(padded)
    rows = turned[pl.ds(pl.multiple_of(first - base, 8), rows_dev), :width]
    for copy in range(copies):
        pack(mine_ref.at[copy], rows)


def ladder_kernel(
    occ_block, sizes, pair_ref, after_ref, amp_hbm, vec_hbm, out_ref,
    weight, left_even, left_odd, amp_t, vectors, total, sem,
):
    _, width, rows_all = vectors.shape
    lefts = (left_even, left_odd)
    starts = [sum(sizes[:c]) for c in range(len(sizes))]
    irrep = irrep_of(pair_ref, lax.axis_index("tile"), occ_block)
    pieces = [(q, 1) for q in range(sizes[0])] + list(zip(starts[1:], sizes[1:]))
    load_amp = pltpu.make_async_copy(amp_hbm, amp_t, sem.at[len(pieces)])
    load_amp.start()
    loads = [
        pltpu.make_async_copy(
            vec_hbm.at[pl.ds(begin, size)], vectors.at[pl.ds(begin, size)], sem.at[index]
        )
        for index, (begin, size) in enumerate(pieces)
    ]
    for load in loads:
        load.start()
    weight[...] = jnp.zeros_like(weight)
    fill = jnp.zeros((LANES - width, rows_all), jnp.bfloat16)

    def prepare(c, q):
        for half, part in enumerate(split(vectors[starts[c] + q])):
            lefts[c % 2][q, :, half * LANES : (half + 1) * LANES] = jnp.transpose(
                jnp.concatenate([part, fill], axis=0)
            )

    def beside(parts):
        return jnp.concatenate(parts, axis=1)

    def first(c, block):
        size = sizes[c]
        rows = lefts[c % 2][:size, block * width : (block + 1) * width, :]
        both = jnp.dot(
            rows.reshape(size * width, 2 * LANES),
            weight[block],
            preferred_element_type=jnp.float32,
        )
        parts = split(both[:, :LANES] + both[:, LANES:])
        return jnp.concatenate(
            [beside([x[q * width : (q + 1) * width] for q in range(size)]) for x in parts], axis=0
        )

    def second(c, block, middle):
        size = sizes[c]
        begin = pl.multiple_of(lax.bitwise_xor(block, irrep) * width, 16)
        rows = lefts[c % 2][:size, pl.ds(begin, width), :]
        other = jnp.concatenate(
            [
                beside([rows[q, :, h * LANES : (h + 1) * LANES] for q in range(size)])
                for h in range(2)
            ],
            axis=0,
        )
        value = lax.dot_general(
            middle, other, (((1,), (1,)), ((), ())), preferred_element_type=jnp.float32
        )
        total[block] = value if c == 0 else total[block] + value

    load_amp.wait()
    amp = jnp.transpose(amp_t[...])
    for block in range(8):
        high, low = split(amp[block * width : (block + 1) * width, :])
        for row in (0, LANES):
            weight[block, row : row + width, :width] = high
            weight[block, row : row + width, LANES : LANES + width] = low
    for q in range(sizes[0]):
        loads[q].wait()
        prepare(0, q)
    work = [(c, block) for c in range(len(sizes)) for block in range(8)]
    middle = first(*work[0])
    for index, (c, block) in enumerate(work):
        if c + 1 < len(sizes):
            size = sizes[c + 1]
            if block == 0:
                loads[sizes[0] + c].wait()
            for q in range(block * size // 8, (block + 1) * size // 8):
                prepare(c + 1, q)
        following = first(*work[index + 1]) if index + 1 < len(work) else None
        second(c, block, middle)
        middle = following
    half = width // 2
    for block in range(8):
        value = (
            total[block, :width, :width]
            + total[block, :width, width:]
            + total[block, width:, :width]
            + total[block, width:, width:]
        )
        for part in range(2):
            piece = 2 * block + part
            pack(out_ref.at[piece], value[part * half : (part + 1) * half])


def hole_kernel(occ_block, pair_ref, integral_ref, rows_ref, *out_refs):
    me = lax.axis_index("tile")
    my_z, my_y = lax.div(me, Y), lax.rem(me, Y)
    near = lax.div(my_z, NEAR) * NEAR
    count = rows_ref.shape[0]
    sources = [(near + i // Y) * Y + i % Y for i in range(count)]
    irreps = [irrep_of(pair_ref, source, occ_block) for source in sources]
    for step, out_ref in enumerate(out_refs):
        target = lax.bitwise_xor(my_z, NEAR * step) * Y + my_y
        irrep = irrep_of(pair_ref, target, occ_block)
        value = None
        for i in range(count):
            factor = jnp.where(irrep == irreps[i], integral_ref[target, sources[i]], 0.0)
            term = factor * rows_ref[i]
            value = term if value is None else value + term
        out_ref[...] = value


def final_kernel(occ_block, pair_ref, occ_ref, vir_ref, other_ref, ladder_ref, *refs):
    out_ref = refs[-1]
    pair = lax.axis_index("tile")
    slab = lax.axis_index("slab")
    rows, width = out_ref.shape
    irrep = irrep_of(pair_ref, pair, occ_block)
    block = lax.div(slab, 2)
    moved = ladder_ref[0]
    for piece in range(1, ladder_ref.shape[0]):
        moved = moved + ladder_ref[piece]
    for hole_ref in refs[:-1]:
        moved = moved + hole_ref[...]
    residual = other_ref[...] + unpack(moved, width)
    pair_energy = occ_ref[pair_ref[0, pair]] + occ_ref[pair_ref[1, pair]]
    column = vir_ref[pl.ds(lax.bitwise_xor(block, irrep), 1), :]
    own = vir_ref[pl.ds(block, 1), :]
    lane = lax.broadcasted_iota(jnp.int32, (rows, width), 1)
    row = lax.broadcasted_iota(jnp.int32, (rows, width), 0) + lax.rem(slab, 2) * rows
    row_energy = jnp.sum(jnp.where(lane == row, own, 0.0), axis=1, keepdims=True)
    out_ref[...] = residual / (pair_energy - row_energy - column)


def local(amplitudes, cholesky, pair_occ, hole_integrals, other_terms, occ_energy, vir_energy):
    _, rows_all, width = amplitudes.shape
    vectors = cholesky.shape[0]
    slabs = lax.axis_size("slab")
    tiles = lax.axis_size("tile")
    rows_dev = rows_all // slabs
    depth = tiles // Y
    packed = (rows_dev - 8, LANES)
    occ_block = occ_energy.shape[0] // 8
    vmem = pl.BlockSpec(memory_space=pltpu.VMEM)
    smem = pl.BlockSpec(memory_space=pltpu.SMEM)
    classes = depth // NEAR
    groups = [
        [(far * NEAR + near) * Y + y for near in range(NEAR) for y in range(Y)]
        for far in range(classes)
    ]

    hbm = pl.BlockSpec(memory_space=pltpu.MemorySpace.HBM)
    small = pltpu.CompilerParams(vmem_limit_bytes=6 << 20)
    pairs = jnp.transpose(pair_occ)
    amp_t = jnp.transpose(amplitudes[0])
    vectors_t = jnp.transpose(cholesky, (0, 2, 1))

    mine = pl.pallas_call(
        head_kernel,
        out_shape=jax.ShapeDtypeStruct((NEAR * Y,) + packed, jnp.float32),
        in_specs=[hbm],
        out_specs=vmem,
        scratch_shapes=[
            pltpu.VMEM((width, 2 * LANES), jnp.float32),
            pltpu.VMEM((2 * LANES, LANES), jnp.float32),
            pltpu.SemaphoreType.DMA,
        ],
        compiler_params=pltpu.CompilerParams(vmem_limit_bytes=60 << 20),
        name="head",
    )(amp_t)
    gathered = lax.all_to_all(mine, "tile", 0, 0, axis_index_groups=groups, tiled=True)

    sizes = SIZES
    flops = 2 * vectors * 8 * width * (2 * LANES) * (2 * LANES) * 2
    ladder = pl.pallas_call(
        functools.partial(ladder_kernel, occ_block, sizes),
        out_shape=jax.ShapeDtypeStruct((slabs,) + packed, jnp.float32),
        in_specs=[smem, hbm, hbm, hbm],
        out_specs=vmem,
        scratch_shapes=[
            pltpu.VMEM((8, 2 * LANES, 2 * LANES), jnp.bfloat16),
            pltpu.VMEM((max(sizes[::2]), rows_all, 2 * LANES), jnp.bfloat16),
            pltpu.VMEM((max(sizes[1::2]), rows_all, 2 * LANES), jnp.bfloat16),
            pltpu.VMEM((width, rows_all), jnp.float32),
            pltpu.VMEM((vectors, width, rows_all), jnp.float32),
            pltpu.VMEM((8, 2 * width, 2 * width), jnp.float32),
            pltpu.SemaphoreType.DMA((sizes[0] + len(sizes),)),
        ],
        compiler_params=pltpu.CompilerParams(vmem_limit_bytes=58 << 20),
        cost_estimate=pl.CostEstimate(
            flops=flops, bytes_accessed=cholesky.size * 4, transcendentals=0
        ),
        name="ladder",
    )(pairs, mine, amp_t, vectors_t)
    pieces = lax.all_to_all(ladder, "slab", 0, 0, tiled=True)
    gathered, _ = lax.optimization_barrier((gathered, ladder))
    partial = pl.pallas_call(
        functools.partial(hole_kernel, occ_block),
        out_shape=[jax.ShapeDtypeStruct(packed, jnp.float32)] * classes,
        in_specs=[smem, smem, vmem],
        out_specs=[vmem] * classes,
        compiler_params=small,
        name="hole",
    )(pairs, hole_integrals, gathered)
    hole = [partial[0]]
    for step in range(1, classes):
        route = [(z * Y + y, (z ^ (NEAR * step)) * Y + y) for z in range(depth) for y in range(Y)]
        hole.append(lax.ppermute(partial[step], "tile", route))
    out = pl.pallas_call(
        functools.partial(final_kernel, occ_block),
        out_shape=jax.ShapeDtypeStruct((rows_dev, width), jnp.float32),
        in_specs=[smem, smem] + [vmem] * (3 + classes),
        out_specs=vmem,
        compiler_params=small,
        name="final",
    )(pairs, occ_energy, vir_energy.reshape(8, width), other_terms[0], pieces, *hole)
    return out[None]


def solution(mesh):
    placed = (
        P("tile", None, None),
        P("slab", None, None),
        P(),
        P(),
        P("tile", "slab", None),
        P(),
        P(),
    )
    return jax.shard_map(
        local, mesh=mesh, in_specs=placed, out_specs=P("tile", "slab", None), check_vma=False
    )
```

```python
import functools

import jax
import jax.numpy as jnp
from jax import lax
from jax.experimental import pallas as pl
from jax.experimental.pallas import tpu as pltpu
from jax.sharding import PartitionSpec as P

LANES = 128
Y = 8
SIZES = (2, 6, 8, 8, 8)
NEAR = 2


def split(x):
    high = x.astype(jnp.bfloat16)
    return high, (x - high.astype(jnp.float32)).astype(jnp.bfloat16)


def irrep_of(pair_ref, pair, occ_block):
    return lax.bitwise_xor(
        lax.div(pair_ref[0, pair], occ_block), lax.div(pair_ref[1, pair], occ_block)
    )


def pack(ref, rows):
    height, width = rows.shape
    spare = LANES - width
    ref[:, width:] = jnp.zeros((height - 8, spare), jnp.float32)
    ref[:, :width] = rows[: height - 8]
    for part in range(width // spare):
        ref[part * 8 : part * 8 + 8, width:] = rows[
            height - 8 :, part * spare : (part + 1) * spare
        ]


def unpack(tile, width):
    spare = LANES - width
    last = [tile[part * 8 : part * 8 + 8, width:] for part in range(width // spare)]
    return jnp.concatenate([tile[:, :width], jnp.concatenate(last, axis=1)], axis=0)


def head_kernel(amp_t_ref, mine_ref, window, turned, sem):
    width, rows_all = amp_t_ref.shape
    copies = mine_ref.shape[0]
    rows_dev = mine_ref.shape[1] + 8
    span = window.shape[1]
    first = lax.axis_index("slab") * rows_dev
    base = jnp.minimum(lax.div(first, LANES) * LANES, rows_all - span)
    load = pltpu.make_async_copy(
        amp_t_ref.at[:, pl.ds(pl.multiple_of(base, LANES), span)], window, sem
    )
    load.start()
    load.wait()
    padded = jnp.concatenate(
        [window[...], jnp.zeros((LANES - width, span), jnp.float32)], axis=0
    )
    turned[...] = jnp.transpose(padded)
    rows = turned[pl.ds(pl.multiple_of(first - base, 8), rows_dev), :width]
    for copy in range(copies):
        pack(mine_ref.at[copy], rows)


def ladder_kernel(
    occ_block, sizes, pair_ref, after_ref, amp_hbm, vec_hbm, out_ref,
    weight, left_even, left_odd, amp_t, vectors, total, sem,
):
    _, width, rows_all = vectors.shape
    lefts = (left_even, left_odd)
    starts = [sum(sizes[:c]) for c in range(len(sizes))]
    irrep = irrep_of(pair_ref, lax.axis_index("tile"), occ_block)
    pieces = [(q, 1) for q in range(sizes[0])] + list(zip(starts[1:], sizes[1:]))
    load_amp = pltpu.make_async_copy(amp_hbm, amp_t, sem.at[len(pieces)])
    load_amp.start()
    loads = [
        pltpu.make_async_copy(
            vec_hbm.at[pl.ds(begin, size)], vectors.at[pl.ds(begin, size)], sem.at[index]
        )
        for index, (begin, size) in enumerate(pieces)
    ]
    for load in loads:
        load.start()
    weight[...] = jnp.zeros_like(weight)
    fill = jnp.zeros((LANES - width, rows_all), jnp.bfloat16)

    def prepare(c, q):
        for half, part in enumerate(split(vectors[starts[c] + q])):
            lefts[c % 2][q, :, half * LANES : (half + 1) * LANES] = jnp.transpose(
                jnp.concatenate([part, fill], axis=0)
            )

    def beside(parts):
        return jnp.concatenate(parts, axis=1)

    def first(c, block):
        size = sizes[c]
        rows = lefts[c % 2][:size, block * width : (block + 1) * width, :]
        both = jnp.dot(
            rows.reshape(size * width, 2 * LANES),
            weight[block],
            preferred_element_type=jnp.float32,
        )
        parts = split(both[:, :LANES] + both[:, LANES:])
        return jnp.concatenate(
            [beside([x[q * width : (q + 1) * width] for q in range(size)]) for x in parts], axis=0
        )

    def second(c, block, middle):
        size = sizes[c]
        begin = pl.multiple_of(lax.bitwise_xor(block, irrep) * width, 16)
        rows = lefts[c % 2][:size, pl.ds(begin, width), :]
        other = jnp.concatenate(
            [
                beside([rows[q, :, h * LANES : (h + 1) * LANES] for q in range(size)])
                for h in range(2)
            ],
            axis=0,
        )
        value = lax.dot_general(
            middle, other, (((1,), (1,)), ((), ())), preferred_element_type=jnp.float32
        )
        total[block] = value if c == 0 else total[block] + value

    load_amp.wait()
    amp = jnp.transpose(amp_t[...])
    for block in range(8):
        high, low = split(amp[block * width : (block + 1) * width, :])
        for row in (0, LANES):
            weight[block, row : row + width, :width] = high
            weight[block, row : row + width, LANES : LANES + width] = low
    for q in range(sizes[0]):
        loads[q].wait()
        prepare(0, q)
    work = [(c, block) for c in range(len(sizes)) for block in range(8)]
    middle = first(*work[0])
    for index, (c, block) in enumerate(work):
        if c + 1 < len(sizes):
            size = sizes[c + 1]
            if block == 0:
                loads[sizes[0] + c].wait()
            for q in range(block * size // 8, (block + 1) * size // 8):
                prepare(c + 1, q)
        following = first(*work[index + 1]) if index + 1 < len(work) else None
        second(c, block, middle)
        middle = following
    half = width // 2
    for block in range(8):
        value = (
            total[block, :width, :width]
            + total[block, :width, width:]
            + total[block, width:, :width]
            + total[block, width:, width:]
        )
        for part in range(2):
            piece = 2 * block + part
            pack(out_ref.at[piece], value[part * half : (part + 1) * half])


def hole_kernel(occ_block, pair_ref, integral_ref, rows_ref, *out_refs):
    me = lax.axis_index("tile")
    my_z, my_y = lax.div(me, Y), lax.rem(me, Y)
    near = lax.div(my_z, NEAR) * NEAR
    count = rows_ref.shape[0]
    sources = [(near + i // Y) * Y + i % Y for i in range(count)]
    irreps = [irrep_of(pair_ref, source, occ_block) for source in sources]
    for step, out_ref in enumerate(out_refs):
        target = lax.bitwise_xor(my_z, NEAR * step) * Y + my_y
        irrep = irrep_of(pair_ref, target, occ_block)
        value = None
        for i in range(count):
            factor = jnp.where(irrep == irreps[i], integral_ref[target, sources[i]], 0.0)
            term = factor * rows_ref[i]
            value = term if value is None else value + term
        out_ref[...] = value


def final_kernel(occ_block, pair_ref, occ_ref, vir_ref, other_ref, ladder_ref, *refs):
    out_ref = refs[-1]
    pair = lax.axis_index("tile")
    slab = lax.axis_index("slab")
    rows, width = out_ref.shape
    irrep = irrep_of(pair_ref, pair, occ_block)
    block = lax.div(slab, 2)
    moved = ladder_ref[0]
    for piece in range(1, ladder_ref.shape[0]):
        moved = moved + ladder_ref[piece]
    for hole_ref in refs[:-1]:
        moved = moved + hole_ref[...]
    residual = other_ref[...] + unpack(moved, width)
    pair_energy = occ_ref[pair_ref[0, pair]] + occ_ref[pair_ref[1, pair]]
    column = vir_ref[pl.ds(lax.bitwise_xor(block, irrep), 1), :]
    own = vir_ref[pl.ds(block, 1), :]
    lane = lax.broadcasted_iota(jnp.int32, (rows, width), 1)
    row = lax.broadcasted_iota(jnp.int32, (rows, width), 0) + lax.rem(slab, 2) * rows
    row_energy = jnp.sum(jnp.where(lane == row, own, 0.0), axis=1, keepdims=True)
    out_ref[...] = residual / (pair_energy - row_energy - column)


def local(amplitudes, cholesky, pair_occ, hole_integrals, other_terms, occ_energy, vir_energy):
    _, rows_all, width = amplitudes.shape
    vectors = cholesky.shape[0]
    slabs = lax.axis_size("slab")
    tiles = lax.axis_size("tile")
    rows_dev = rows_all // slabs
    depth = tiles // Y
    packed = (rows_dev - 8, LANES)
    occ_block = occ_energy.shape[0] // 8
    vmem = pl.BlockSpec(memory_space=pltpu.VMEM)
    smem = pl.BlockSpec(memory_space=pltpu.SMEM)
    classes = depth // NEAR
    groups = [
        [(far * NEAR + near) * Y + y for near in range(NEAR) for y in range(Y)]
        for far in range(classes)
    ]

    hbm = pl.BlockSpec(memory_space=pltpu.MemorySpace.HBM)
    small = pltpu.CompilerParams(vmem_limit_bytes=6 << 20)
    pairs = jnp.transpose(pair_occ)
    amp_t = jnp.transpose(amplitudes[0])
    vectors_t = jnp.transpose(cholesky, (0, 2, 1))

    mine = pl.pallas_call(
        head_kernel,
        out_shape=jax.ShapeDtypeStruct((NEAR * Y,) + packed, jnp.float32),
        in_specs=[hbm],
        out_specs=vmem,
        scratch_shapes=[
            pltpu.VMEM((width, 2 * LANES), jnp.float32),
            pltpu.VMEM((2 * LANES, LANES), jnp.float32),
            pltpu.SemaphoreType.DMA,
        ],
        compiler_params=pltpu.CompilerParams(vmem_limit_bytes=60 << 20),
        name="head",
    )(amp_t)
    gathered = lax.all_to_all(mine, "tile", 0, 0, axis_index_groups=groups, tiled=True)

    sizes = SIZES
    flops = 2 * vectors * 8 * width * (2 * LANES) * (2 * LANES) * 2
    ladder = pl.pallas_call(
        functools.partial(ladder_kernel, occ_block, sizes),
        out_shape=jax.ShapeDtypeStruct((slabs,) + packed, jnp.float32),
        in_specs=[smem, hbm, hbm, hbm],
        out_specs=vmem,
        scratch_shapes=[
            pltpu.VMEM((8, 2 * LANES, 2 * LANES), jnp.bfloat16),
            pltpu.VMEM((max(sizes[::2]), rows_all, 2 * LANES), jnp.bfloat16),
            pltpu.VMEM((max(sizes[1::2]), rows_all, 2 * LANES), jnp.bfloat16),
            pltpu.VMEM((width, rows_all), jnp.float32),
            pltpu.VMEM((vectors, width, rows_all), jnp.float32),
            pltpu.VMEM((8, 2 * width, 2 * width), jnp.float32),
            pltpu.SemaphoreType.DMA((sizes[0] + len(sizes),)),
        ],
        compiler_params=pltpu.CompilerParams(vmem_limit_bytes=58 << 20),
        cost_estimate=pl.CostEstimate(
            flops=flops, bytes_accessed=cholesky.size * 4, transcendentals=0
        ),
        name="ladder",
    )(pairs, mine, amp_t, vectors_t)
    pieces = lax.all_to_all(ladder, "slab", 0, 0, tiled=True)
    gathered, _ = lax.optimization_barrier((gathered, ladder))
    partial = pl.pallas_call(
        functools.partial(hole_kernel, occ_block),
        out_shape=[jax.ShapeDtypeStruct(packed, jnp.float32)] * classes,
        in_specs=[smem, smem, vmem],
        out_specs=[vmem] * classes,
        compiler_params=small,
        name="hole",
    )(pairs, hole_integrals, gathered)
    hole = [partial[0]]
    for step in sorted(range(1, classes), key=lambda step: min(step, classes - step)):
        route = [(z * Y + y, (z ^ (NEAR * step)) * Y + y) for z in range(depth) for y in range(Y)]
        hole.append(lax.ppermute(partial[step], "tile", route))
    out = pl.pallas_call(
        functools.partial(final_kernel, occ_block),
        out_shape=jax.ShapeDtypeStruct((rows_dev, width), jnp.float32),
        in_specs=[smem, smem] + [vmem] * (3 + classes),
        out_specs=vmem,
        compiler_params=small,
        name="final",
    )(pairs, occ_energy, vir_energy.reshape(8, width), other_terms[0], pieces, *hole)
    return out[None]


def solution(mesh):
    placed = (
        P("tile", None, None),
        P("slab", None, None),
        P(),
        P(),
        P("tile", "slab", None),
        P(),
        P(),
    )
    return jax.shard_map(
        local, mesh=mesh, in_specs=placed, out_specs=P("tile", "slab", None), check_vma=False
    )
```

```python
import functools

import jax
import jax.numpy as jnp
from jax import lax
from jax.experimental import pallas as pl
from jax.experimental.pallas import tpu as pltpu
from jax.sharding import PartitionSpec as P

LANES = 128
Y = 8
SIZES = (2, 6, 8, 8, 8)
NEAR = 2


def split(x):
    high = x.astype(jnp.bfloat16)
    return high, (x - high.astype(jnp.float32)).astype(jnp.bfloat16)


def irrep_of(pair_ref, pair, occ_block):
    return lax.bitwise_xor(
        lax.div(pair_ref[0, pair], occ_block), lax.div(pair_ref[1, pair], occ_block)
    )


def pack(ref, rows):
    height, width = rows.shape
    spare = LANES - width
    ref[:, width:] = jnp.zeros((height - 8, spare), jnp.float32)
    ref[:, :width] = rows[: height - 8]
    for part in range(width // spare):
        ref[part * 8 : part * 8 + 8, width:] = rows[
            height - 8 :, part * spare : (part + 1) * spare
        ]


def unpack(tile, width):
    spare = LANES - width
    last = [tile[part * 8 : part * 8 + 8, width:] for part in range(width // spare)]
    return jnp.concatenate([tile[:, :width], jnp.concatenate(last, axis=1)], axis=0)


def head_kernel(amp_t_ref, mine_ref, window, turned, sem):
    width, rows_all = amp_t_ref.shape
    copies = mine_ref.shape[0]
    rows_dev = mine_ref.shape[1] + 8
    span = window.shape[1]
    first = lax.axis_index("slab") * rows_dev
    base = jnp.minimum(lax.div(first, LANES) * LANES, rows_all - span)
    load = pltpu.make_async_copy(
        amp_t_ref.at[:, pl.ds(pl.multiple_of(base, LANES), span)], window, sem
    )
    load.start()
    load.wait()
    padded = jnp.concatenate(
        [window[...], jnp.zeros((LANES - width, span), jnp.float32)], axis=0
    )
    turned[...] = jnp.transpose(padded)
    rows = turned[pl.ds(pl.multiple_of(first - base, 8), rows_dev), :width]
    for copy in range(copies):
        pack(mine_ref.at[copy], rows)


def ladder_kernel(
    occ_block, sizes, pair_ref, after_ref, amp_hbm, vec_hbm, out_hbm,
    weight, left_even, left_odd, amp_t, vectors, total, out_ref, sem, out_sem,
):
    _, width, rows_all = vectors.shape
    lefts = (left_even, left_odd)
    starts = [sum(sizes[:c]) for c in range(len(sizes))]
    irrep = irrep_of(pair_ref, lax.axis_index("tile"), occ_block)
    pieces = [(q, 1) for q in range(sizes[0])] + list(zip(starts[1:], sizes[1:]))
    load_amp = pltpu.make_async_copy(amp_hbm, amp_t, sem.at[len(pieces)])
    load_amp.start()
    loads = [
        pltpu.make_async_copy(
            vec_hbm.at[pl.ds(begin, size)], vectors.at[pl.ds(begin, size)], sem.at[index]
        )
        for index, (begin, size) in enumerate(pieces)
    ]
    for load in loads:
        load.start()
    weight[...] = jnp.zeros_like(weight)
    fill = jnp.zeros((LANES - width, rows_all), jnp.bfloat16)

    def prepare(c, q):
        for half, part in enumerate(split(vectors[starts[c] + q])):
            lefts[c % 2][q, :, half * LANES : (half + 1) * LANES] = jnp.transpose(
                jnp.concatenate([part, fill], axis=0)
            )

    def beside(parts):
        return jnp.concatenate(parts, axis=1)

    def first(c, block):
        size = sizes[c]
        rows = lefts[c % 2][:size, block * width : (block + 1) * width, :]
        both = jnp.dot(
            rows.reshape(size * width, 2 * LANES),
            weight[block],
            preferred_element_type=jnp.float32,
        )
        parts = split(both[:, :LANES] + both[:, LANES:])
        return jnp.concatenate(
            [beside([x[q * width : (q + 1) * width] for q in range(size)]) for x in parts], axis=0
        )

    def second(c, block, middle):
        size = sizes[c]
        begin = pl.multiple_of(lax.bitwise_xor(block, irrep) * width, 16)
        rows = lefts[c % 2][:size, pl.ds(begin, width), :]
        other = jnp.concatenate(
            [
                beside([rows[q, :, h * LANES : (h + 1) * LANES] for q in range(size)])
                for h in range(2)
            ],
            axis=0,
        )
        value = lax.dot_general(
            middle, other, (((1,), (1,)), ((), ())), preferred_element_type=jnp.float32
        )
        total[block] = value if c == 0 else total[block] + value

    def store(block):
        part = pl.ds(2 * block, 2)
        return pltpu.make_async_copy(out_ref.at[part], out_hbm.at[part], out_sem.at[block])

    def finish(block):
        half = width // 2
        value = (
            total[block, :width, :width]
            + total[block, :width, width:]
            + total[block, width:, :width]
            + total[block, width:, width:]
        )
        for part in range(2):
            pack(out_ref.at[2 * block + part], value[part * half : (part + 1) * half])
        store(block).start()

    load_amp.wait()
    amp = jnp.transpose(amp_t[...])
    for block in range(8):
        high, low = split(amp[block * width : (block + 1) * width, :])
        for row in (0, LANES):
            weight[block, row : row + width, :width] = high
            weight[block, row : row + width, LANES : LANES + width] = low
    for q in range(sizes[0]):
        loads[q].wait()
        prepare(0, q)
    work = [(c, block) for c in range(len(sizes)) for block in range(8)]
    middle = first(*work[0])
    for index, (c, block) in enumerate(work):
        if c + 1 < len(sizes):
            size = sizes[c + 1]
            if block == 0:
                loads[sizes[0] + c].wait()
            for q in range(block * size // 8, (block + 1) * size // 8):
                prepare(c + 1, q)
        following = first(*work[index + 1]) if index + 1 < len(work) else None
        second(c, block, middle)
        middle = following
        if c + 1 == len(sizes):
            finish(block)
    for block in range(8):
        store(block).wait()


def hole_kernel(occ_block, pair_ref, integral_ref, rows_ref, *out_refs):
    me = lax.axis_index("tile")
    my_z, my_y = lax.div(me, Y), lax.rem(me, Y)
    near = lax.div(my_z, NEAR) * NEAR
    count = rows_ref.shape[0]
    sources = [(near + i // Y) * Y + i % Y for i in range(count)]
    irreps = [irrep_of(pair_ref, source, occ_block) for source in sources]
    for step, out_ref in enumerate(out_refs):
        target = lax.bitwise_xor(my_z, NEAR * step) * Y + my_y
        irrep = irrep_of(pair_ref, target, occ_block)
        value = None
        for i in range(count):
            factor = jnp.where(irrep == irreps[i], integral_ref[target, sources[i]], 0.0)
            term = factor * rows_ref[i]
            value = term if value is None else value + term
        out_ref[...] = value


def final_kernel(occ_block, pair_ref, occ_ref, vir_ref, other_ref, ladder_ref, *refs):
    out_ref = refs[-1]
    pair = lax.axis_index("tile")
    slab = lax.axis_index("slab")
    rows, width = out_ref.shape
    irrep = irrep_of(pair_ref, pair, occ_block)
    block = lax.div(slab, 2)
    moved = ladder_ref[0]
    for piece in range(1, ladder_ref.shape[0]):
        moved = moved + ladder_ref[piece]
    for hole_ref in refs[:-1]:
        moved = moved + hole_ref[...]
    residual = other_ref[...] + unpack(moved, width)
    pair_energy = occ_ref[pair_ref[0, pair]] + occ_ref[pair_ref[1, pair]]
    column = vir_ref[pl.ds(lax.bitwise_xor(block, irrep), 1), :]
    own = vir_ref[pl.ds(block, 1), :]
    lane = lax.broadcasted_iota(jnp.int32, (rows, width), 1)
    row = lax.broadcasted_iota(jnp.int32, (rows, width), 0) + lax.rem(slab, 2) * rows
    row_energy = jnp.sum(jnp.where(lane == row, own, 0.0), axis=1, keepdims=True)
    out_ref[...] = residual / (pair_energy - row_energy - column)


def local(amplitudes, cholesky, pair_occ, hole_integrals, other_terms, occ_energy, vir_energy):
    _, rows_all, width = amplitudes.shape
    vectors = cholesky.shape[0]
    slabs = lax.axis_size("slab")
    tiles = lax.axis_size("tile")
    rows_dev = rows_all // slabs
    depth = tiles // Y
    packed = (rows_dev - 8, LANES)
    occ_block = occ_energy.shape[0] // 8
    vmem = pl.BlockSpec(memory_space=pltpu.VMEM)
    smem = pl.BlockSpec(memory_space=pltpu.SMEM)
    classes = depth // NEAR
    groups = [
        [(far * NEAR + near) * Y + y for near in range(NEAR) for y in range(Y)]
        for far in range(classes)
    ]

    hbm = pl.BlockSpec(memory_space=pltpu.MemorySpace.HBM)
    small = pltpu.CompilerParams(vmem_limit_bytes=6 << 20)
    pairs = jnp.transpose(pair_occ)
    amp_t = jnp.transpose(amplitudes[0])
    vectors_t = jnp.transpose(cholesky, (0, 2, 1))

    mine = pl.pallas_call(
        head_kernel,
        out_shape=jax.ShapeDtypeStruct((NEAR * Y,) + packed, jnp.float32),
        in_specs=[hbm],
        out_specs=vmem,
        scratch_shapes=[
            pltpu.VMEM((width, 2 * LANES), jnp.float32),
            pltpu.VMEM((2 * LANES, LANES), jnp.float32),
            pltpu.SemaphoreType.DMA,
        ],
        compiler_params=pltpu.CompilerParams(vmem_limit_bytes=60 << 20),
        name="head",
    )(amp_t)
    gathered = lax.all_to_all(mine, "tile", 0, 0, axis_index_groups=groups, tiled=True)

    sizes = SIZES
    flops = 2 * vectors * 8 * width * (2 * LANES) * (2 * LANES) * 2
    ladder = pl.pallas_call(
        functools.partial(ladder_kernel, occ_block, sizes),
        out_shape=jax.ShapeDtypeStruct((slabs,) + packed, jnp.float32),
        in_specs=[smem, hbm, hbm, hbm],
        out_specs=hbm,
        scratch_shapes=[
            pltpu.VMEM((8, 2 * LANES, 2 * LANES), jnp.bfloat16),
            pltpu.VMEM((max(sizes[::2]), rows_all, 2 * LANES), jnp.bfloat16),
            pltpu.VMEM((max(sizes[1::2]), rows_all, 2 * LANES), jnp.bfloat16),
            pltpu.VMEM((width, rows_all), jnp.float32),
            pltpu.VMEM((vectors, width, rows_all), jnp.float32),
            pltpu.VMEM((8, 2 * width, 2 * width), jnp.float32),
            pltpu.VMEM((slabs,) + packed, jnp.float32),
            pltpu.SemaphoreType.DMA((sizes[0] + len(sizes),)),
            pltpu.SemaphoreType.DMA((8,)),
        ],
        compiler_params=pltpu.CompilerParams(vmem_limit_bytes=58 << 20),
        cost_estimate=pl.CostEstimate(
            flops=flops, bytes_accessed=cholesky.size * 4, transcendentals=0
        ),
        name="ladder",
    )(pairs, mine, amp_t, vectors_t)
    pieces = lax.all_to_all(ladder, "slab", 0, 0, tiled=True)
    gathered, _ = lax.optimization_barrier((gathered, ladder))
    partial = pl.pallas_call(
        functools.partial(hole_kernel, occ_block),
        out_shape=[jax.ShapeDtypeStruct(packed, jnp.float32)] * classes,
        in_specs=[smem, smem, vmem],
        out_specs=[vmem] * classes,
        compiler_params=small,
        name="hole",
    )(pairs, hole_integrals, gathered)
    hole = [partial[0]]
    for step in sorted(range(1, classes), key=lambda step: min(step, classes - step)):
        route = [(z * Y + y, (z ^ (NEAR * step)) * Y + y) for z in range(depth) for y in range(Y)]
        hole.append(lax.ppermute(partial[step], "tile", route))
    out = pl.pallas_call(
        functools.partial(final_kernel, occ_block),
        out_shape=jax.ShapeDtypeStruct((rows_dev, width), jnp.float32),
        in_specs=[smem, smem] + [vmem] * (3 + classes),
        out_specs=vmem,
        compiler_params=small,
        name="final",
    )(pairs, occ_energy, vir_energy.reshape(8, width), other_terms[0], pieces, *hole)
    return out[None]


def solution(mesh):
    placed = (
        P("tile", None, None),
        P("slab", None, None),
        P(),
        P(),
        P("tile", "slab", None),
        P(),
        P(),
    )
    return jax.shard_map(
        local, mesh=mesh, in_specs=placed, out_specs=P("tile", "slab", None), check_vma=False
    )
```

```python
import functools

import jax
import jax.numpy as jnp
from jax import lax
from jax.experimental import pallas as pl
from jax.experimental.pallas import tpu as pltpu
from jax.sharding import PartitionSpec as P

LANES = 128
Y = 8
SIZES = (2, 6, 8, 8, 8)
NEAR = 2


def split(x):
    high = x.astype(jnp.bfloat16)
    return high, (x - high.astype(jnp.float32)).astype(jnp.bfloat16)


def irrep_of(pair_ref, pair, occ_block):
    return lax.bitwise_xor(
        lax.div(pair_ref[0, pair], occ_block), lax.div(pair_ref[1, pair], occ_block)
    )


def pack(ref, rows):
    height, width = rows.shape
    spare = LANES - width
    ref[:, width:] = jnp.zeros((height - 8, spare), jnp.float32)
    ref[:, :width] = rows[: height - 8]
    for part in range(width // spare):
        ref[part * 8 : part * 8 + 8, width:] = rows[
            height - 8 :, part * spare : (part + 1) * spare
        ]


def unpack(tile, width):
    spare = LANES - width
    last = [tile[part * 8 : part * 8 + 8, width:] for part in range(width // spare)]
    return jnp.concatenate([tile[:, :width], jnp.concatenate(last, axis=1)], axis=0)


def head_kernel(amp_t_ref, mine_ref, window, turned, sem):
    width, rows_all = amp_t_ref.shape
    copies = mine_ref.shape[0]
    rows_dev = mine_ref.shape[1] + 8
    span = window.shape[1]
    first = lax.axis_index("slab") * rows_dev
    base = jnp.minimum(lax.div(first, LANES) * LANES, rows_all - span)
    load = pltpu.make_async_copy(
        amp_t_ref.at[:, pl.ds(pl.multiple_of(base, LANES), span)], window, sem
    )
    load.start()
    load.wait()
    padded = jnp.concatenate(
        [window[...], jnp.zeros((LANES - width, span), jnp.float32)], axis=0
    )
    turned[...] = jnp.transpose(padded)
    rows = turned[pl.ds(pl.multiple_of(first - base, 8), rows_dev), :width]
    for copy in range(copies):
        pack(mine_ref.at[copy], rows)


def ladder_kernel(
    occ_block, sizes, pair_ref, after_ref, amp_hbm, vec_hbm, out_ref,
    weight, left_even, left_odd, amp_t, vectors, total, sem,
):
    _, width, rows_all = vectors.shape
    lefts = (left_even, left_odd)
    starts = [sum(sizes[:c]) for c in range(len(sizes))]
    irrep = irrep_of(pair_ref, lax.axis_index("tile"), occ_block)
    pieces = [(q, 1) for q in range(sizes[0])] + list(zip(starts[1:], sizes[1:]))
    load_amp = pltpu.make_async_copy(amp_hbm, amp_t, sem.at[len(pieces)])
    loads = [
        pltpu.make_async_copy(
            vec_hbm.at[pl.ds(begin, size)], vectors.at[pl.ds(begin, size)], sem.at[index]
        )
        for index, (begin, size) in enumerate(pieces)
    ]
    for load in loads[: sizes[0]] + [load_amp] + loads[sizes[0] :]:
        load.start()
    weight[...] = jnp.zeros_like(weight)
    fill = jnp.zeros((LANES - width, rows_all), jnp.bfloat16)

    def prepare(c, q):
        for half, part in enumerate(split(vectors[starts[c] + q])):
            lefts[c % 2][q, :, half * LANES : (half + 1) * LANES] = jnp.transpose(
                jnp.concatenate([part, fill], axis=0)
            )

    def beside(parts):
        return jnp.concatenate(parts, axis=1)

    def first(c, block):
        size = sizes[c]
        rows = lefts[c % 2][:size, block * width : (block + 1) * width, :]
        both = jnp.dot(
            rows.reshape(size * width, 2 * LANES),
            weight[block],
            preferred_element_type=jnp.float32,
        )
        parts = split(both[:, :LANES] + both[:, LANES:])
        return jnp.concatenate(
            [beside([x[q * width : (q + 1) * width] for q in range(size)]) for x in parts], axis=0
        )

    def second(c, block, middle):
        size = sizes[c]
        begin = pl.multiple_of(lax.bitwise_xor(block, irrep) * width, 16)
        rows = lefts[c % 2][:size, pl.ds(begin, width), :]
        other = jnp.concatenate(
            [
                beside([rows[q, :, h * LANES : (h + 1) * LANES] for q in range(size)])
                for h in range(2)
            ],
            axis=0,
        )
        value = lax.dot_general(
            middle, other, (((1,), (1,)), ((), ())), preferred_element_type=jnp.float32
        )
        total[block] = value if c == 0 else total[block] + value

    for q in range(sizes[0]):
        loads[q].wait()
        prepare(0, q)
    load_amp.wait()
    amp = jnp.transpose(amp_t[...])
    for block in range(8):
        high, low = split(amp[block * width : (block + 1) * width, :])
        for row in (0, LANES):
            weight[block, row : row + width, :width] = high
            weight[block, row : row + width, LANES : LANES + width] = low
    work = [(c, block) for c in range(len(sizes)) for block in range(8)]
    middle = first(*work[0])
    for index, (c, block) in enumerate(work):
        if c + 1 < len(sizes):
            size = sizes[c + 1]
            if block == 0:
                loads[sizes[0] + c].wait()
            for q in range(block * size // 8, (block + 1) * size // 8):
                prepare(c + 1, q)
        following = first(*work[index + 1]) if index + 1 < len(work) else None
        second(c, block, middle)
        middle = following
    half = width // 2
    for block in range(8):
        value = (
            total[block, :width, :width]
            + total[block, :width, width:]
            + total[block, width:, :width]
            + total[block, width:, width:]
        )
        for part in range(2):
            piece = 2 * block + part
            pack(out_ref.at[piece], value[part * half : (part + 1) * half])


def hole_kernel(occ_block, pair_ref, integral_ref, rows_ref, *out_refs):
    me = lax.axis_index("tile")
    my_z, my_y = lax.div(me, Y), lax.rem(me, Y)
    near = lax.div(my_z, NEAR) * NEAR
    count = rows_ref.shape[0]
    sources = [(near + i // Y) * Y + i % Y for i in range(count)]
    irreps = [irrep_of(pair_ref, source, occ_block) for source in sources]
    for step, out_ref in enumerate(out_refs):
        target = lax.bitwise_xor(my_z, NEAR * step) * Y + my_y
        irrep = irrep_of(pair_ref, target, occ_block)
        value = None
        for i in range(count):
            factor = jnp.where(irrep == irreps[i], integral_ref[target, sources[i]], 0.0)
            term = factor * rows_ref[i]
            value = term if value is None else value + term
        out_ref[...] = value


def final_kernel(occ_block, pair_ref, occ_ref, vir_ref, other_ref, ladder_ref, *refs):
    out_ref = refs[-1]
    pair = lax.axis_index("tile")
    slab = lax.axis_index("slab")
    rows, width = out_ref.shape
    irrep = irrep_of(pair_ref, pair, occ_block)
    block = lax.div(slab, 2)
    moved = ladder_ref[0]
    for piece in range(1, ladder_ref.shape[0]):
        moved = moved + ladder_ref[piece]
    for hole_ref in refs[:-1]:
        moved = moved + hole_ref[...]
    residual = other_ref[...] + unpack(moved, width)
    pair_energy = occ_ref[pair_ref[0, pair]] + occ_ref[pair_ref[1, pair]]
    column = vir_ref[pl.ds(lax.bitwise_xor(block, irrep), 1), :]
    own = vir_ref[pl.ds(block, 1), :]
    lane = lax.broadcasted_iota(jnp.int32, (rows, width), 1)
    row = lax.broadcasted_iota(jnp.int32, (rows, width), 0) + lax.rem(slab, 2) * rows
    row_energy = jnp.sum(jnp.where(lane == row, own, 0.0), axis=1, keepdims=True)
    out_ref[...] = residual / (pair_energy - row_energy - column)


def local(amplitudes, cholesky, pair_occ, hole_integrals, other_terms, occ_energy, vir_energy):
    _, rows_all, width = amplitudes.shape
    vectors = cholesky.shape[0]
    slabs = lax.axis_size("slab")
    tiles = lax.axis_size("tile")
    rows_dev = rows_all // slabs
    depth = tiles // Y
    packed = (rows_dev - 8, LANES)
    occ_block = occ_energy.shape[0] // 8
    vmem = pl.BlockSpec(memory_space=pltpu.VMEM)
    smem = pl.BlockSpec(memory_space=pltpu.SMEM)
    classes = depth // NEAR
    groups = [
        [(far * NEAR + near) * Y + y for near in range(NEAR) for y in range(Y)]
        for far in range(classes)
    ]

    hbm = pl.BlockSpec(memory_space=pltpu.MemorySpace.HBM)
    small = pltpu.CompilerParams(vmem_limit_bytes=6 << 20)
    pairs = jnp.transpose(pair_occ)
    amp_t = jnp.transpose(amplitudes[0])
    vectors_t = jnp.transpose(cholesky, (0, 2, 1))

    mine = pl.pallas_call(
        head_kernel,
        out_shape=jax.ShapeDtypeStruct((NEAR * Y,) + packed, jnp.float32),
        in_specs=[hbm],
        out_specs=vmem,
        scratch_shapes=[
            pltpu.VMEM((width, 2 * LANES), jnp.float32),
            pltpu.VMEM((2 * LANES, LANES), jnp.float32),
            pltpu.SemaphoreType.DMA,
        ],
        compiler_params=pltpu.CompilerParams(vmem_limit_bytes=60 << 20),
        name="head",
    )(amp_t)
    gathered = lax.all_to_all(mine, "tile", 0, 0, axis_index_groups=groups, tiled=True)

    sizes = SIZES
    flops = 2 * vectors * 8 * width * (2 * LANES) * (2 * LANES) * 2
    ladder = pl.pallas_call(
        functools.partial(ladder_kernel, occ_block, sizes),
        out_shape=jax.ShapeDtypeStruct((slabs,) + packed, jnp.float32),
        in_specs=[smem, hbm, hbm, hbm],
        out_specs=vmem,
        scratch_shapes=[
            pltpu.VMEM((8, 2 * LANES, 2 * LANES), jnp.bfloat16),
            pltpu.VMEM((max(sizes[::2]), rows_all, 2 * LANES), jnp.bfloat16),
            pltpu.VMEM((max(sizes[1::2]), rows_all, 2 * LANES), jnp.bfloat16),
            pltpu.VMEM((width, rows_all), jnp.float32),
            pltpu.VMEM((vectors, width, rows_all), jnp.float32),
            pltpu.VMEM((8, 2 * width, 2 * width), jnp.float32),
            pltpu.SemaphoreType.DMA((sizes[0] + len(sizes),)),
        ],
        compiler_params=pltpu.CompilerParams(vmem_limit_bytes=58 << 20),
        cost_estimate=pl.CostEstimate(
            flops=flops, bytes_accessed=cholesky.size * 4, transcendentals=0
        ),
        name="ladder",
    )(pairs, mine, amp_t, vectors_t)
    pieces = lax.all_to_all(ladder, "slab", 0, 0, tiled=True)
    gathered, _ = lax.optimization_barrier((gathered, ladder))
    partial = pl.pallas_call(
        functools.partial(hole_kernel, occ_block),
        out_shape=[jax.ShapeDtypeStruct(packed, jnp.float32)] * classes,
        in_specs=[smem, smem, vmem],
        out_specs=[vmem] * classes,
        compiler_params=small,
        name="hole",
    )(pairs, hole_integrals, gathered)
    hole = [partial[0]]
    for step in sorted(range(1, classes), key=lambda step: min(step, classes - step)):
        route = [(z * Y + y, (z ^ (NEAR * step)) * Y + y) for z in range(depth) for y in range(Y)]
        hole.append(lax.ppermute(partial[step], "tile", route))
    out = pl.pallas_call(
        functools.partial(final_kernel, occ_block),
        out_shape=jax.ShapeDtypeStruct((rows_dev, width), jnp.float32),
        in_specs=[smem, smem] + [vmem] * (3 + classes),
        out_specs=vmem,
        compiler_params=small,
        name="final",
    )(pairs, occ_energy, vir_energy.reshape(8, width), other_terms[0], pieces, *hole)
    return out[None]


def solution(mesh):
    placed = (
        P("tile", None, None),
        P("slab", None, None),
        P(),
        P(),
        P("tile", "slab", None),
        P(),
        P(),
    )
    return jax.shard_map(
        local, mesh=mesh, in_specs=placed, out_specs=P("tile", "slab", None), check_vma=False
    )
```
